256 devices in a mesh: col: 16 (over x, y), row: 8 (over z), pair: 2 (over core).
Axes of the slice: x: 4, y: 4, z: 8, core: 2. Of those that a mesh axis runs over, the one named last changes fastest.
Arguments:
- tokens: bfloat16 [2, 8192, 2880], P(None, ('col', 'row')), may hold values from -6 to 6
- expert_ids: int32 [2, 8192, 4], P(None, ('col', 'row')), may hold values from 0 to 127, all different within a row; in each aligned block of 64 rows (0 to 63, 64 to 127, ..., all dimensions but the last counted through in order) at most 3 rows name the same one
- gate_weights: float32 [2, 8192, 4], P(None, ('col', 'row')), may hold values from 0.05 to 0.6
- migration: int32 [32, 2], replicated, may hold values from 0 to 127, as said below
- up_values: bfloat16 [128, 2880, 1536], P(('col', 'row'), None, 'pair'), may hold values from -0.109375 to 0.109375
- up_scales: bfloat16 [128, 90, 1536], P(('col', 'row'), None, 'pair'), may hold values from 0.3984375 to 2.5
- down_values: bfloat16 [128, 1536, 2880], P(('col', 'row'), 'pair'), may hold values from -0.15625 to 0.15625
- down_scales: bfloat16 [128, 48, 2880], P(('col', 'row'), 'pair'), may hold values from 0.3984375 to 2.5
Outputs:
- mixed: bfloat16 [2, 8192, 2880], P(None, ('col', 'row'), 'pair')
The draws below stay inside these ranges and needn't reach their ends.
Inputs may be any that keep to these rules, and one draw needn't show every extreme that they name: `expert_ids`: each token names 4 different experts. Among one group's 64 tokens of one batch (an aligned block of rows), no expert is named more than 3 times, a bound that some block reaches. `migration`: column 0 names 32 different experts; column 1 names the same experts in another order, none in its own row's place.
All inputs are finite; a program needn't handle non-finite values.
Results may differ from the reference program's by a relative error of at most 0.0077.
Values may be sent and summed in bfloat16 or wider, within the bound.
No kernel may reach another device: no remote copies, remote signals or barrier semaphores. Data moves between devices by JAX's collectives and lax.ppermute only.
A program may use at most 128 MiB of HBM per device.

```python
import math
import jax
import jax.numpy as jnp
import numpy as np
from jax import lax

D = 2880
HW = 1536
TOP = 4
BATCHES = 2
TOK_DEV = 64
EXPERTS = 128
TOKENS = 8192
CAP = 3
MOVED = 32
N_PAIR = 2


def draw_migration(key, part):
    first_key = jax.random.fold_in(key, 11)
    second_key = jax.random.fold_in(key, 23)
    middle = 1 + jax.random.permutation(first_key, EXPERTS - 2)[:MOVED - 2].astype(jnp.int32)
    chosen = jnp.concatenate([jnp.array([0, EXPERTS - 1], dtype=jnp.int32), middle])
    arrangement = jax.random.permutation(second_key, MOVED)
    chosen = chosen[arrangement]
    return jnp.stack([chosen, jnp.roll(chosen, 1)], axis=1)


def block_levels(rng, extent, split, low, high):
    def one(axis_at, shards_of):
        heights = jax.random.uniform(jax.random.fold_in(jax.random.fold_in(rng, 6), axis_at), (shards_of,), jnp.float32, low / len(split), high / len(split))
        return jnp.repeat(jnp.exp(heights), extent[axis_at] // shards_of).reshape((-1,) + (1,) * (len(extent) - axis_at - 1))

    gain = one(*split[0])
    for cut in split[1:]:
        gain = gain * one(*cut)
    return gain


def shared_out(own_key, own, number, rows, count, top, limit, lean):
    order = jax.random.permutation(own_key, count)
    crowded, usual = load_shares(count, rows * top, limit, lean, True), load_shares(count, rows * top, limit, lean, False)
    places = jnp.arange(count)

    def named(sizes, turn):
        used = int((sizes > 0).sum())
        fixed = max(1, used // 4)
        moved = fixed + (places - fixed + turn * (used - fixed)) % max(1, count - fixed)
        return jnp.zeros((count,), jnp.int32).at[order[jnp.where(places < fixed, places, moved)]].set(jnp.asarray(sizes, jnp.int32))

    sizes = jnp.where(number % 4 == 0, named(crowded, number // 4), named(usual, number - number // 4 - 1))
    mixed = jax.random.permutation(jax.random.fold_in(own, 3), count)
    donor, receiver = mixed[0:count // 2 * 2:2], mixed[1:count // 2 * 2:2]
    margin = jnp.minimum(sizes[donor] - 1, limit - sizes[receiver]) // 2
    margin = jnp.where((donor == order[0]) | (receiver == order[0]) | (sizes[receiver] == 0), 0, jnp.maximum(margin, 0))
    moved = jax.random.randint(jax.random.fold_in(own, 4), (count // 2,), 0, 1 << 20) % (margin + 1)
    sizes = sizes.at[donor].add(-moved).at[receiver].add(moved)
    members = jnp.searchsorted(jnp.cumsum(sizes), jnp.arange(rows * top), side="right").astype(jnp.int32)
    table = members.reshape(top, rows).T
    table = table[jax.random.permutation(jax.random.fold_in(own, 1), rows)]
    turn = jax.random.randint(jax.random.fold_in(own, 2), (rows, 1), 0, top)
    return jnp.take_along_axis(table, (jnp.arange(top)[None, :] + turn) % top, axis=1)


def load_shares(amount, total, reach, slope, full):
    portions = [(1 << 20) // math.isqrt(standing ** slope) + 1 for standing in range(1, amount + 1)]
    largest = reach if full else min(reach, max(-(-total // amount), total * portions[0] // sum(portions)))
    least = 1 if total - largest >= amount - 1 else 0
    counts, surplus = [largest] + [least] * (amount - 1), total - largest - least * (amount - 1)
    while surplus > 0:
        free = [i for i in range(1, amount) if counts[i] < largest] or [i for i in range(1, amount) if counts[i] < reach]
        pool, budget = sum([portions[i] for i in free]), surplus
        for i in free:
            extra = min(reach - counts[i], max(1, budget * portions[i] // pool), surplus)
            counts[i] = counts[i] + extra
            surplus = surplus - extra
    return np.array(counts)


def centred(stream_key, extent, width, reach, shards=(), kind=jnp.bfloat16):
    drawn = jax.random.normal(stream_key, extent, jnp.float32) * width
    if len(shards) > 0:
        drawn = block_levels(stream_key, extent, shards, -0.22, 0.18) * drawn
    return jnp.clip(drawn, min=-reach, max=reach).astype(kind)


def setup_inputs(seed: int = 0) -> dict:
    splits = jax.random.split(jax.random.key(seed), 9)
    tokens = centred(splits[0], (BATCHES, TOKENS, D), 1.0, 6.0, ((1, 128),))
    expert_ids_keys = jax.random.split(jax.random.fold_in(splits[1], 1), BATCHES * TOKENS // TOK_DEV)
    expert_ids_turns = jax.random.permutation(jax.random.fold_in(splits[1], 3), BATCHES * TOKENS // TOK_DEV)
    expert_ids = jax.vmap(lambda own, number: shared_out(jax.random.fold_in(splits[1], 2), own, number, TOK_DEV, EXPERTS, TOP, CAP, 2))(expert_ids_keys, expert_ids_turns).reshape((BATCHES, TOKENS, TOP))
    gate_weights = jnp.clip(0.05 + 0.55 * jax.random.uniform(splits[2], (BATCHES, TOKENS, TOP), jnp.float32) ** block_levels(splits[2], (BATCHES, TOKENS, TOP), ((1, 128),), -0.2, 0.2), 0.05, 0.6)
    migration = draw_migration(jax.random.fold_in(splits[8], 71), 0)
    up_values = centred(splits[4], (EXPERTS, D, HW), D ** -0.5, 0.109375, ((0, 128), (2, 2)))
    up_scales = jnp.clip(jnp.exp(math.log(2.5) - 1.8364954 * jax.random.uniform(splits[5], (EXPERTS, D // 32, HW), jnp.float32) ** block_levels(splits[5], (EXPERTS, D // 32, HW), ((0, 128), (2, 2)), -0.2, 0.2)), 0.3984375, 2.5).astype(jnp.bfloat16)
    down_values = centred(splits[6], (EXPERTS, HW, D), HW ** -0.5, 0.15625, ((0, 128), (1, 2)))
    down_scales = jnp.clip(jnp.exp(math.log(2.5) - 1.8364954 * jax.random.uniform(splits[7], (EXPERTS, HW // 32, D), jnp.float32) ** block_levels(splits[7], (EXPERTS, HW // 32, D), ((0, 128), (1, 2)), -0.2, 0.2)), 0.3984375, 2.5).astype(jnp.bfloat16)
    return {"tokens": tokens, "expert_ids": expert_ids, "gate_weights": gate_weights, "migration": migration, "up_values": up_values, "up_scales": up_scales, "down_values": down_values, "down_scales": down_scales}


def dequantize(values, scales):
    wide_scales = jnp.repeat(scales, 32, axis=0)
    return (values.astype(jnp.float32) * wide_scales.astype(jnp.float32)).astype(jnp.bfloat16)


def activate(pre_act):
    return pre_act * jax.nn.sigmoid(1.702 * pre_act)


def slot_tables(route_ids, gate_rows):
    devices = route_ids.shape[0] // TOK_DEV
    flat_ids = route_ids.reshape(devices, TOK_DEV * TOP)
    onehot = (flat_ids[:, :, None] == jnp.arange(EXPERTS, dtype=jnp.int32)[None, None, :]).astype(jnp.int32)
    before = jnp.cumsum(onehot, axis=1) - onehot
    slot_index = jnp.sum(before * onehot, axis=2)
    owner_index = jnp.arange(devices, dtype=jnp.int32)[:, None]
    position = (owner_index * EXPERTS + flat_ids) * CAP + slot_index
    token_index = (jnp.arange(devices * TOK_DEV * TOP, dtype=jnp.int32) // TOP).reshape(devices, TOK_DEV * TOP)
    index_table = jnp.zeros((devices * EXPERTS * CAP,), jnp.int32).at[position.reshape(-1)].set(token_index.reshape(-1))
    weight_table = jnp.zeros((devices * EXPERTS * CAP,), jnp.float32).at[position.reshape(-1)].set(gate_rows.reshape(-1))
    return index_table.reshape(devices, EXPERTS, CAP), weight_table.reshape(devices, EXPERTS, CAP)


def one_batch(inputs, route_ids, gate_rows, sources, up_values, up_scales, down_values, down_scales):
    index_table, weight_table = slot_tables(route_ids, gate_rows)
    halves = HW // N_PAIR

    def per_expert(running, expert):
        anchor = sources[expert]
        row_index = index_table[:, expert, :].reshape(-1)
        weights = weight_table[:, expert, :].reshape(-1)
        up_weight = dequantize(up_values[anchor], up_scales[anchor])
        down_weight = dequantize(down_values[anchor], down_scales[anchor])
        pre_act = jnp.dot(inputs[row_index], up_weight, preferred_element_type=jnp.float32)
        hidden = activate(pre_act).astype(jnp.bfloat16)
        summed = jnp.zeros((row_index.shape[0], D), jnp.float32)
        for half_index in range(N_PAIR):
            partial_value = jnp.dot(hidden[:, half_index * halves:(half_index + 1) * halves],
                              down_weight[half_index * halves:(half_index + 1) * halves],
                              preferred_element_type=jnp.float32).astype(jnp.bfloat16)
            partial_value = lax.optimization_barrier(partial_value)
            summed = summed + partial_value.astype(jnp.float32)
        expert_out = lax.optimization_barrier(summed.astype(jnp.bfloat16)).astype(jnp.float32)
        return running.at[row_index].add(weights[:, None] * expert_out), None

    running, _ = lax.scan(per_expert, jnp.zeros((TOKENS, D), jnp.float32), jnp.arange(EXPERTS, dtype=jnp.int32))
    return running.astype(jnp.bfloat16)


def reference(tokens, expert_ids, gate_weights, migration, up_values, up_scales, down_values, down_scales):
    slot_ids = jnp.arange(EXPERTS, dtype=jnp.int32)
    matches = (migration[None, :, 1] == slot_ids[:, None]).astype(jnp.int32)
    moved_sources = slot_ids + jnp.sum(matches * (migration[None, :, 0] - slot_ids[:, None]), axis=1)
    first_out = one_batch(tokens[0], expert_ids[0], gate_weights[0], slot_ids,
                          up_values, up_scales, down_values, down_scales)
    second = one_batch(tokens[1], expert_ids[1], gate_weights[1], moved_sources,
                       up_values, up_scales, down_values, down_scales)
    return jnp.stack([first_out, second], axis=0)
```

```python
import jax
import jax.numpy as jnp
from jax import lax
from jax.experimental import pallas as pl
from jax.experimental.pallas import tpu as pltpu
from jax.sharding import PartitionSpec as P

D = 2880
HALF = D // 2
HW2 = 768
E = 128
TOK = 64
TOP = 4
SUB = 8
LANES = 1152
THIRD = 384
WIDE = 1536
CHUNK = 256
BF = jnp.bfloat16
F32 = jnp.float32


def iota(shape, dim):
    return lax.broadcasted_iota(jnp.int32, shape, dim)


def one_hot(cond, dtype=BF):
    return jnp.where(cond, 1.0, 0.0).astype(dtype)


def dot(a, b, ca=1, cb=0):
    return lax.dot_general(a, b, (((ca,), (cb,)), ((), ())), preferred_element_type=F32)


def wanted(p, b, i):
    q = jnp.where(p < 6, p, 3 * (p - 6) + i)
    return jnp.where(b == (q & 1) + jnp.where(p < 6, 0, 2), (q >> 1) + 1, -1).astype(F32)


def placement(h, mig):
    named_from = one_hot(mig[0:1, :] == iota((E, mig.shape[1]), 0))
    named_to = one_hot(mig[1:2, :] == iota((E, mig.shape[1]), 0))
    moved = dot(named_from, named_to, 1, 1)
    named = dot(jnp.ones((SUB, mig.shape[1]), BF), named_to, 1, 1)[0:1, :]
    eye = one_hot(iota((E, E), 0) == iota((E, E), 1), F32)
    hf = h.astype(F32)
    return (moved * hf + eye * (1.0 - hf * named)).astype(BF)


def slot_codes(place, ids):
    owner = jnp.zeros((E, TOK), F32)
    for k in range(TOP):
        owner = owner + one_hot(ids[k : k + 1, :] == iota((E, TOK), 0), F32)
    named = dot(place, owner.astype(BF)).astype(BF)
    earlier = one_hot(iota((TOK, TOK), 0) < iota((TOK, TOK), 1))
    rank = dot(named, earlier)
    return (named.astype(F32) * (rank + 1.0)).astype(BF)


def third(ref, i):
    return ref.at[:, i * THIRD : (i + 1) * THIRD]


def pack_body(h_ref, ids_ref, mig_ref, tok_ref, out_ref, zero_ref, tok, tail, rows, sems):
    h = h_ref[0]
    load = pltpu.make_async_copy(tok_ref.at[h], tok, sems.at[3])
    load.start()
    zero_ref[...] = jnp.zeros(zero_ref.shape, BF)
    codes = slot_codes(placement(h, mig_ref[...]), ids_ref[h])
    repeat = one_hot((iota((TOK, 4 * TOK), 1) & (TOK - 1)) == iota((TOK, 4 * TOK), 0))
    spread = one_hot((iota((E * SUB, E), 0) >> 3) == iota((E * SUB, E), 1))
    codes = dot(spread, dot(codes, repeat).astype(BF)).reshape(E, SUB, 4 * TOK)
    p = iota((SUB, 4 * TOK), 0)
    b = iota((SUB, 4 * TOK), 1) >> 6
    load.wait()
    left = D - WIDE - LANES
    tail[:, 0:left] = tok[:, WIDE + LANES : D]
    tail[:, left:THIRD] = jnp.zeros((TOK, THIRD - left), BF)
    stores = []
    for i in range(3):
        select = one_hot(codes == wanted(p, b, i)[None]).reshape(E * SUB, 4 * TOK)
        source = jnp.concatenate(
            [
                tok[:, i * THIRD : (i + 1) * THIRD],
                tok[:, WIDE + i * THIRD : WIDE + (i + 1) * THIRD],
                tok[:, LANES:WIDE],
                tail[...],
            ],
            axis=0,
        )
        rows[:, i * THIRD : (i + 1) * THIRD] = dot(select, source).astype(BF)
        stores.append(pltpu.make_async_copy(third(rows, i), third(out_ref, i), sems.at[i]))
        stores[i].start()
    for store in stores:
        store.wait()


VMEM = pl.BlockSpec(memory_space=pltpu.VMEM)
SMEM = pl.BlockSpec(memory_space=pltpu.SMEM)
ANY = pl.BlockSpec(memory_space=pl.ANY)


def pack(h, ids, mig, tokens):
    return pl.pallas_call(
        pack_body,
        in_specs=[SMEM, VMEM, VMEM, ANY],
        out_specs=[ANY, VMEM],
        scratch_shapes=[
            pltpu.VMEM((TOK, D), BF),
            pltpu.VMEM((TOK, THIRD), BF),
            pltpu.VMEM((E * SUB, LANES), BF),
            pltpu.SemaphoreType.DMA((4,)),
        ],
        out_shape=[
            jax.ShapeDtypeStruct((E * SUB, LANES), BF),
            jax.ShapeDtypeStruct((16, 128), BF),
        ],
        name="pack",
        compiler_params=pltpu.CompilerParams(vmem_limit_bytes=24 << 20),
    )(h, ids, mig, tokens)


def mix_body(h_ref, ids_ref, mig_ref, gates_ref, out_ref):
    ids = ids_ref[h_ref[0]]
    gates = gates_ref[h_ref[0]]
    place = placement(h_ref[0], mig_ref[...])
    codes = slot_codes(place, ids)
    gate = jnp.zeros((E, TOK), F32)
    for k in range(TOP):
        gate = gate + jnp.where(ids[k : k + 1, :] == iota((E, TOK), 0), gates[k : k + 1, :], 0.0)
    high = gate.astype(BF)
    low = (gate - high.astype(F32)).astype(BF)
    repeat = one_hot((iota((4 * TOK, TOK), 0) & (TOK - 1)) == iota((4 * TOK, TOK), 1))
    spread = one_hot((iota((E, E * SUB), 1) >> 3) == iota((E, E * SUB), 0))

    def widened(x):
        return dot(dot(repeat, x, 1, 1).astype(BF), spread)

    codes = widened(codes)
    high = widened(dot(place, high).astype(BF))
    low = widened(dot(place, low).astype(BF))
    p = iota((4 * TOK, E * SUB), 1) & (SUB - 1)
    b = iota((4 * TOK, E * SUB), 0) >> 6
    for i in range(3):
        hit = codes == wanted(p, b, i)
        out_ref[i, 0 : 4 * TOK, :] = jnp.where(hit, high, 0.0).astype(BF)
        out_ref[i, 4 * TOK : 8 * TOK, :] = jnp.where(hit, low, 0.0).astype(BF)


def mix_weights(h, ids, mig, gates):
    return pl.pallas_call(
        mix_body,
        in_specs=[SMEM, VMEM, VMEM, VMEM],
        out_specs=VMEM,
        out_shape=jax.ShapeDtypeStruct((3, 8 * TOK, E * SUB), BF),
        name="mix_weights",
        compiler_params=pltpu.CompilerParams(vmem_limit_bytes=24 << 20),
    )(h, ids, mig, gates)


def pieces():
    for q in range(6):
        j, g = q // 2, q % 2
        for part in range(WIDE // 128):
            if part < 9:
                yield j, g * WIDE + part * 128, part, q
            else:
                yield j, g * WIDE + part * 128, 3 * (q % 3) + part - 9, 6 + q // 3


def expert_body(
    in_ref, up_a_hbm, up_b_hbm, down_a_hbm, down_b_hbm, out_hbm,
    wide, rows, hidden, out_ref, up_a, up_b, down_a, down_b, up_sems, down_sems, out_sems,
):
    ups, downs, stores = [], [], []
    for n, (src, dst) in enumerate(((up_a_hbm, up_a), (up_b_hbm, up_b))):
        for c in range(HW2 // CHUNK):
            cut = (slice(None), pl.ds(c * CHUNK, CHUNK))
            ups.append(pltpu.make_async_copy(src.at[cut], dst.at[cut], up_sems.at[len(ups)]))
    for n, (src, dst) in enumerate(((down_a_hbm, down_a), (down_b_hbm, down_b))):
        downs.append(pltpu.make_async_copy(src, dst, down_sems.at[n]))
    for load in ups + downs:
        load.start()
    for part in range(LANES // 128):
        wide[part] = in_ref[:, part * 128 : (part + 1) * 128].astype(F32)
    for j, lane, part, p in pieces():
        rows[j * E : (j + 1) * E, lane : lane + 128] = wide[part, pl.ds(p, E, stride=SUB), :].astype(BF)
    for n, up_ref in enumerate((up_a, up_b)):
        for c in range(HW2 // CHUNK):
            ups[n * (HW2 // CHUNK) + c].wait()
            pre = dot(rows[:, 0:D], up_ref[:, c * CHUNK : (c + 1) * CHUNK])
            act = pre / (1.0 + jnp.exp(-1.702 * pre))
            hidden[:, n * HW2 + c * CHUNK : n * HW2 + (c + 1) * CHUNK] = act.astype(BF)

    for load in downs:
        load.wait()

    def down(n0, n1):
        return dot(hidden[:, 0:HW2], down_a[n0:n1, :], 1, 1) + dot(hidden[:, HW2 : 2 * HW2], down_b[n0:n1, :], 1, 1)

    for g in range(2):
        y = down(g * HALF + LANES, (g + 1) * HALF)
        for j in range(3):
            q = 2 * j + g
            mine = y[j * E : (j + 1) * E]
            to = pl.ds(6 + q // 3, E, stride=SUB)
            wide[3 * (q % 3), to, :] = mine[:, 0:128]
            wide[3 * (q % 3) + 1, to, :] = mine[:, 128:256]
            last = jnp.concatenate([mine[:, 256:288], jnp.zeros((E, 96), F32)], axis=1)
            wide[3 * (q % 3) + 2, to, :] = last
    for i in range(3):
        for g in range(2):
            y = down(g * HALF + i * THIRD, g * HALF + (i + 1) * THIRD)
            for j in range(3):
                for part in range(3):
                    mine = y[j * E : (j + 1) * E, part * 128 : (part + 1) * 128]
                    wide[3 * i + part, pl.ds(2 * j + g, E, stride=SUB), :] = mine
        for part in range(3 * i, 3 * i + 3):
            out_ref[:, part * 128 : (part + 1) * 128] = wide[part].astype(BF)
        stores.append(pltpu.make_async_copy(third(out_ref, i), third(out_hbm, i), out_sems.at[i]))
        stores[i].start()
    for store in stores:
        store.wait()


def on_chip(x):
    return pltpu.with_memory_space_constraint(x, pltpu.VMEM)


def expert(received, up_a, up_b, down_a, down_b):
    return pl.pallas_call(
        expert_body,
        in_specs=[VMEM, ANY, ANY, ANY, ANY],
        out_specs=ANY,
        scratch_shapes=[
            pltpu.VMEM((LANES // 128, E * SUB, 128), F32),
            pltpu.VMEM((3 * E, 2 * WIDE), BF),
            pltpu.VMEM((3 * E, 2 * HW2), BF),
            pltpu.VMEM((E * SUB, LANES), BF),
        ]
        + [pltpu.VMEM((D, HW2), BF)] * 4
        + [pltpu.SemaphoreType.DMA((2 * HW2 // CHUNK,)), pltpu.SemaphoreType.DMA((2,)), pltpu.SemaphoreType.DMA((3,))],
        out_shape=jax.ShapeDtypeStruct((E * SUB, LANES), BF),
        name="expert",
        compiler_params=pltpu.CompilerParams(vmem_limit_bytes=44 << 20),
    )(on_chip(received), up_a, up_b, down_a, down_b)


def combine_body(h_ref, weights_ref, in_ref, full_ref, send_ref):
    h = h_ref[0]
    mains, tail = [], 0.0
    for i in range(3):
        out = dot(weights_ref[i], in_ref[:, i * THIRD : (i + 1) * THIRD])
        out = out[0 : 4 * TOK] + out[4 * TOK : 8 * TOK]
        mains.append(out[0 : 2 * TOK])
        tail = tail + out[2 * TOK : 4 * TOK]
    for g in range(2):
        own = slice(g * TOK, (g + 1) * TOK)

        def put(ref, own=own):
            for i in range(3):
                ref[:, i * THIRD : (i + 1) * THIRD] = mains[i][own].astype(BF)
            ref[:, LANES:HALF] = tail[own, 0 : HALF - LANES].astype(BF)

        @pl.when(h == g)
        def _():
            put(full_ref.at[g])

        @pl.when(h != g)
        def _():
            put(send_ref)


def combine(h, weights, returned):
    return pl.pallas_call(
        combine_body,
        in_specs=[SMEM, VMEM, VMEM],
        out_specs=[VMEM, VMEM],
        out_shape=[
            jax.ShapeDtypeStruct((2, TOK, HALF), BF),
            jax.ShapeDtypeStruct((TOK, HALF), BF),
        ],
        name="combine",
        compiler_params=pltpu.CompilerParams(vmem_limit_bytes=24 << 20),
    )(h, weights, on_chip(returned))


def finish_body(h_ref, full_ref, other_ref, out_ref, sem):
    copy = pltpu.make_async_copy(other_ref, out_ref.at[1 - h_ref[0]], sem)
    copy.start()
    copy.wait()


def finish(h, full, other):
    return pl.pallas_call(
        finish_body,
        in_specs=[SMEM, ANY, VMEM],
        out_specs=ANY,
        scratch_shapes=[pltpu.SemaphoreType.DMA(())],
        out_shape=jax.ShapeDtypeStruct(full.shape, BF),
        input_output_aliases={1: 0},
        name="finish",
    )(h, full, on_chip(other))


def exchange(x):
    blocks = x.reshape(E, SUB, LANES)
    return lax.all_to_all(blocks, ("col", "row"), 0, 0, tiled=True).reshape(E * SUB, LANES)


def swapped(x):
    return lax.ppermute(x, "pair", [(0, 1), (1, 0)])


def dequantize_up(values, scales):
    shaped = values.reshape(D // 32, 32, HW2).astype(F32) * scales.astype(F32)[:, None, :]
    return shaped.astype(BF).reshape(D, HW2)


def dequantize_down(values, scales):
    group = (iota((HW2 // 32, HW2), 1) // 32 == iota((HW2 // 32, HW2), 0)).astype(BF)
    spread = jnp.einsum("bn,bk->nk", scales, group, preferred_element_type=F32)
    return (values.T.astype(F32) * spread).astype(BF)


def per_device(
    tokens, expert_ids, gate_weights, migration, up_values, up_scales, down_values, down_scales
):
    own = lax.axis_index("pair")
    h = own.astype(jnp.int32).reshape(1)
    ids = expert_ids.transpose(0, 2, 1)
    gates = gate_weights.transpose(0, 2, 1)
    mig = migration.T
    packed, zero = pack(h, ids, mig, tokens)
    received = exchange(packed)
    up_a = dequantize_up(up_values[0], up_scales[0] + zero[0, 0])
    down_a = dequantize_down(down_values[0], down_scales[0] + zero[0, 0])
    up_b = swapped(up_a)
    down_b = swapped(down_a)
    weights = mix_weights(h, ids, mig, gates)
    returned = exchange(expert(received, up_a, up_b, down_a, down_b))
    full, send = combine(h, weights, returned)
    return finish(h, full, swapped(send))


def solution(mesh):
    placed = (
        P(None, ("col", "row"), None),
        P(None, ("col", "row"), None),
        P(None, ("col", "row"), None),
        P(),
        P(("col", "row"), None, "pair"),
        P(("col", "row"), None, "pair"),
        P(("col", "row"), "pair", None),
        P(("col", "row"), "pair", None),
    )
    return jax.shard_map(
        per_device,
        mesh=mesh,
        in_specs=placed,
        out_specs=P(None, ("col", "row"), "pair"),
        check_vma=False,
    )
```

```python
import jax
import jax.numpy as jnp
from jax import lax
from jax.experimental import pallas as pl
from jax.experimental.pallas import tpu as pltpu
from jax.sharding import PartitionSpec as P

D = 2880
HALF = D // 2
HW2 = 768
E = 128
TOK = 64
TOP = 4
SUB = 8
LANES = 1152
THIRD = 384
WIDE = 1536
CHUNK = 256
BF = jnp.bfloat16
F32 = jnp.float32


def iota(shape, dim):
    return lax.broadcasted_iota(jnp.int32, shape, dim)


def one_hot(cond, dtype=BF):
    return jnp.where(cond, 1.0, 0.0).astype(dtype)


def dot(a, b, ca=1, cb=0):
    return lax.dot_general(a, b, (((ca,), (cb,)), ((), ())), preferred_element_type=F32)


def wanted(p, b, i):
    q = jnp.where(p < 6, p, 3 * (p - 6) + i)
    return jnp.where(b == (q & 1) + jnp.where(p < 6, 0, 2), (q >> 1) + 1, -1).astype(F32)


def placement(h, mig):
    named_from = one_hot(mig[0:1, :] == iota((E, mig.shape[1]), 0))
    named_to = one_hot(mig[1:2, :] == iota((E, mig.shape[1]), 0))
    moved = dot(named_from, named_to, 1, 1)
    named = dot(jnp.ones((SUB, mig.shape[1]), BF), named_to, 1, 1)[0:1, :]
    eye = one_hot(iota((E, E), 0) == iota((E, E), 1), F32)
    hf = h.astype(F32)
    return (moved * hf + eye * (1.0 - hf * named)).astype(BF)


def slot_codes(place, ids):
    owner = jnp.zeros((E, TOK), F32)
    for k in range(TOP):
        owner = owner + one_hot(ids[k : k + 1, :] == iota((E, TOK), 0), F32)
    named = dot(place, owner.astype(BF)).astype(BF)
    earlier = one_hot(iota((TOK, TOK), 0) < iota((TOK, TOK), 1))
    rank = dot(named, earlier)
    return (named.astype(F32) * (rank + 1.0)).astype(BF)


def third(ref, i):
    return ref.at[:, i * THIRD : (i + 1) * THIRD]


def pack_body(h_ref, ids_ref, mig_ref, tok_ref, out_ref, zero_ref, tok, tail, rows, ids, mig, sems):
    h = h_ref[0]
    small = [
        pltpu.make_async_copy(ids_ref.at[h], ids, sems.at[4]),
        pltpu.make_async_copy(mig_ref, mig, sems.at[5]),
    ]
    for copy in small:
        copy.start()
    load = pltpu.make_async_copy(tok_ref.at[h], tok, sems.at[3])
    load.start()
    zero_ref[...] = jnp.zeros(zero_ref.shape, BF)
    for copy in small:
        copy.wait()
    codes = slot_codes(placement(h, mig[...]), ids[...])
    repeat = one_hot((iota((TOK, 4 * TOK), 1) & (TOK - 1)) == iota((TOK, 4 * TOK), 0))
    spread = one_hot((iota((E * SUB, E), 0) >> 3) == iota((E * SUB, E), 1))
    codes = dot(spread, dot(codes, repeat).astype(BF)).reshape(E, SUB, 4 * TOK)
    p = iota((SUB, 4 * TOK), 0)
    b = iota((SUB, 4 * TOK), 1) >> 6
    load.wait()
    left = D - WIDE - LANES
    tail[:, 0:left] = tok[:, WIDE + LANES : D]
    tail[:, left:THIRD] = jnp.zeros((TOK, THIRD - left), BF)
    stores = []
    for i in range(3):
        select = one_hot(codes == wanted(p, b, i)[None]).reshape(E * SUB, 4 * TOK)
        source = jnp.concatenate(
            [
                tok[:, i * THIRD : (i + 1) * THIRD],
                tok[:, WIDE + i * THIRD : WIDE + (i + 1) * THIRD],
                tok[:, LANES:WIDE],
                tail[...],
            ],
            axis=0,
        )
        rows[:, i * THIRD : (i + 1) * THIRD] = dot(select, source).astype(BF)
        stores.append(pltpu.make_async_copy(third(rows, i), third(out_ref, i), sems.at[i]))
        stores[i].start()
    for store in stores:
        store.wait()


VMEM = pl.BlockSpec(memory_space=pltpu.VMEM)
SMEM = pl.BlockSpec(memory_space=pltpu.SMEM)
HBM = pl.BlockSpec(memory_space=pltpu.HBM)


def pack(h, ids, mig, tokens):
    return pl.pallas_call(
        pack_body,
        in_specs=[SMEM, HBM, HBM, HBM],
        out_specs=[HBM, VMEM],
        scratch_shapes=[
            pltpu.VMEM((TOK, D), BF),
            pltpu.VMEM((TOK, THIRD), BF),
            pltpu.VMEM((E * SUB, LANES), BF),
            pltpu.VMEM((TOP, TOK), jnp.int32),
            pltpu.VMEM(mig.shape, jnp.int32),
            pltpu.SemaphoreType.DMA((6,)),
        ],
        out_shape=[
            pltpu.HBM((E * SUB, LANES), BF),
            jax.ShapeDtypeStruct((16, 128), BF),
        ],
        name="pack",
        compiler_params=pltpu.CompilerParams(vmem_limit_bytes=24 << 20),
    )(h, in_hbm(ids), in_hbm(mig), in_hbm(tokens))


def mix_body(h_ref, ids_ref, mig_ref, gates_ref, out_ref):
    ids = ids_ref[h_ref[0]]
    gates = gates_ref[h_ref[0]]
    place = placement(h_ref[0], mig_ref[...])
    codes = slot_codes(place, ids)
    gate = jnp.zeros((E, TOK), F32)
    for k in range(TOP):
        gate = gate + jnp.where(ids[k : k + 1, :] == iota((E, TOK), 0), gates[k : k + 1, :], 0.0)
    high = gate.astype(BF)
    low = (gate - high.astype(F32)).astype(BF)
    repeat = one_hot((iota((4 * TOK, TOK), 0) & (TOK - 1)) == iota((4 * TOK, TOK), 1))
    spread = one_hot((iota((E, E * SUB), 1) >> 3) == iota((E, E * SUB), 0))

    def widened(x):
        return dot(dot(repeat, x, 1, 1).astype(BF), spread)

    codes = widened(codes)
    high = widened(dot(place, high).astype(BF))
    low = widened(dot(place, low).astype(BF))
    p = iota((4 * TOK, E * SUB), 1) & (SUB - 1)
    b = iota((4 * TOK, E * SUB), 0) >> 6
    for i in range(3):
        hit = codes == wanted(p, b, i)
        out_ref[i, 0 : 4 * TOK, :] = jnp.where(hit, high, 0.0).astype(BF)
        out_ref[i, 4 * TOK : 8 * TOK, :] = jnp.where(hit, low, 0.0).astype(BF)


def mix_weights(h, ids, mig, gates):
    return pl.pallas_call(
        mix_body,
        in_specs=[SMEM, VMEM, VMEM, VMEM],
        out_specs=VMEM,
        out_shape=jax.ShapeDtypeStruct((3, 8 * TOK, E * SUB), BF),
        name="mix_weights",
        compiler_params=pltpu.CompilerParams(vmem_limit_bytes=24 << 20),
    )(h, ids, mig, gates)


def pieces():
    for q in range(6):
        j, g = q // 2, q % 2
        for part in range(WIDE // 128):
            if part < 9:
                yield j, g * WIDE + part * 128, part, q
            else:
                yield j, g * WIDE + part * 128, 3 * (q % 3) + part - 9, 6 + q // 3


def expert_body(
    in_ref, up_a_hbm, up_b_hbm, down_a_hbm, down_b_hbm, out_hbm,
    wide, rows, hidden, out_ref, up_a, up_b, down_a, down_b, up_sems, down_sems, out_sems,
):
    ups, downs, stores = [], [], []
    for n, (src, dst) in enumerate(((up_a_hbm, up_a), (up_b_hbm, up_b))):
        for c in range(HW2 // CHUNK):
            cut = (slice(None), pl.ds(c * CHUNK, CHUNK))
            ups.append(pltpu.make_async_copy(src.at[cut], dst.at[cut], up_sems.at[len(ups)]))
    for n, (src, dst) in enumerate(((down_a_hbm, down_a), (down_b_hbm, down_b))):
        downs.append(pltpu.make_async_copy(src, dst, down_sems.at[n]))
    for load in ups + downs:
        load.start()
    for part in range(LANES // 128):
        wide[part] = in_ref[:, part * 128 : (part + 1) * 128].astype(F32)
    for j, lane, part, p in pieces():
        rows[j * E : (j + 1) * E, lane : lane + 128] = wide[part, pl.ds(p, E, stride=SUB), :].astype(BF)
    for n, up_ref in enumerate((up_a, up_b)):
        for c in range(HW2 // CHUNK):
            ups[n * (HW2 // CHUNK) + c].wait()
            pre = dot(rows[:, 0:D], up_ref[:, c * CHUNK : (c + 1) * CHUNK])
            act = pre / (1.0 + jnp.exp(-1.702 * pre))
            hidden[:, n * HW2 + c * CHUNK : n * HW2 + (c + 1) * CHUNK] = act.astype(BF)

    for load in downs:
        load.wait()

    def down(n0, n1):
        return dot(hidden[:, 0:HW2], down_a[n0:n1, :], 1, 1) + dot(hidden[:, HW2 : 2 * HW2], down_b[n0:n1, :], 1, 1)

    def put(y, g, i0, i1):
        for j in range(3):
            for part in range(3 * i0, 3 * i1):
                lane = (part - 3 * i0) * 128
                wide[part, pl.ds(2 * j + g, E, stride=SUB), :] = y[j * E : (j + 1) * E, lane : lane + 128]

    def send(i):
        for part in range(3 * i, 3 * i + 3):
            out_ref[:, part * 128 : (part + 1) * 128] = wide[part].astype(BF)
        stores.append(pltpu.make_async_copy(third(out_ref, i), third(out_hbm, i), out_sems.at[i]))
        stores[-1].start()

    for g in range(2):
        y = down(g * HALF + 2 * THIRD, (g + 1) * HALF)
        put(y, g, 2, 3)
        for j in range(3):
            q = 2 * j + g
            mine = y[j * E : (j + 1) * E, THIRD:]
            to = pl.ds(6 + q // 3, E, stride=SUB)
            wide[3 * (q % 3), to, :] = mine[:, 0:128]
            wide[3 * (q % 3) + 1, to, :] = mine[:, 128:256]
            last = jnp.concatenate([mine[:, 256:288], jnp.zeros((E, 96), F32)], axis=1)
            wide[3 * (q % 3) + 2, to, :] = last
    send(2)
    for g in range(2):
        put(down(g * HALF, g * HALF + 2 * THIRD), g, 0, 2)
    send(0)
    send(1)
    for store in stores:
        store.wait()


def in_hbm(x):
    return pltpu.with_memory_space_constraint(x, pltpu.HBM)


def on_chip(x):
    return pltpu.with_memory_space_constraint(x, pltpu.VMEM)


def expert(received, up_a, up_b, down_a, down_b):
    return pl.pallas_call(
        expert_body,
        in_specs=[VMEM, HBM, HBM, HBM, HBM],
        out_specs=HBM,
        scratch_shapes=[
            pltpu.VMEM((LANES // 128, E * SUB, 128), F32),
            pltpu.VMEM((3 * E, 2 * WIDE), BF),
            pltpu.VMEM((3 * E, 2 * HW2), BF),
            pltpu.VMEM((E * SUB, LANES), BF),
        ]
        + [pltpu.VMEM((D, HW2), BF)] * 4
        + [pltpu.SemaphoreType.DMA((2 * HW2 // CHUNK,)), pltpu.SemaphoreType.DMA((2,)), pltpu.SemaphoreType.DMA((3,))],
        out_shape=pltpu.HBM((E * SUB, LANES), BF),
        name="expert",
        compiler_params=pltpu.CompilerParams(vmem_limit_bytes=44 << 20),
    )(on_chip(received), *[in_hbm(x) for x in (up_a, up_b, down_a, down_b)])


def combine_body(h_ref, weights_ref, in_ref, full_ref, send_ref):
    h = h_ref[0]
    mains, tail = [], 0.0
    for i in range(3):
        out = dot(weights_ref[i], in_ref[:, i * THIRD : (i + 1) * THIRD])
        out = out[0 : 4 * TOK] + out[4 * TOK : 8 * TOK]
        mains.append(out[0 : 2 * TOK])
        tail = tail + out[2 * TOK : 4 * TOK]
    for g in range(2):
        own = slice(g * TOK, (g + 1) * TOK)

        def put(ref, own=own):
            for i in range(3):
                ref[:, i * THIRD : (i + 1) * THIRD] = mains[i][own].astype(BF)
            ref[:, LANES:HALF] = tail[own, 0 : HALF - LANES].astype(BF)

        @pl.when(h == g)
        def _():
            put(full_ref.at[g])

        @pl.when(h != g)
        def _():
            put(send_ref)


def combine(h, weights, returned):
    return pl.pallas_call(
        combine_body,
        in_specs=[SMEM, VMEM, VMEM],
        out_specs=[VMEM, VMEM],
        out_shape=[
            jax.ShapeDtypeStruct((2, TOK, HALF), BF),
            jax.ShapeDtypeStruct((TOK, HALF), BF),
        ],
        name="combine",
        compiler_params=pltpu.CompilerParams(vmem_limit_bytes=24 << 20),
    )(h, weights, on_chip(returned))


def finish_body(h_ref, full_ref, other_ref, out_ref, sem):
    copy = pltpu.make_async_copy(other_ref, out_ref.at[1 - h_ref[0]], sem)
    copy.start()
    copy.wait()


def finish(h, full, other):
    return pl.pallas_call(
        finish_body,
        in_specs=[SMEM, HBM, VMEM],
        out_specs=HBM,
        scratch_shapes=[pltpu.SemaphoreType.DMA(())],
        out_shape=jax.ShapeDtypeStruct(full.shape, BF),
        input_output_aliases={1: 0},
        name="finish",
    )(h, full, on_chip(other))


def exchange(x):
    blocks = x.reshape(E, SUB, LANES)
    return lax.all_to_all(blocks, ("col", "row"), 0, 0, tiled=True).reshape(E * SUB, LANES)


def swapped(x):
    return lax.ppermute(x, "pair", [(0, 1), (1, 0)])


def dequantize_up(values, scales):
    shaped = values.reshape(D // 32, 32, HW2).astype(F32) * scales.astype(F32)[:, None, :]
    return shaped.astype(BF).reshape(D, HW2)


def dequantize_down(values, scales):
    group = (iota((HW2 // 32, HW2), 1) // 32 == iota((HW2 // 32, HW2), 0)).astype(BF)
    spread = jnp.einsum("bn,bk->nk", scales, group, preferred_element_type=F32)
    return (values.T.astype(F32) * spread).astype(BF)


def per_device(
    tokens, expert_ids, gate_weights, migration, up_values, up_scales, down_values, down_scales
):
    own = lax.axis_index("pair")
    h = own.astype(jnp.int32).reshape(1)
    ids = expert_ids.transpose(0, 2, 1)
    gates = gate_weights.transpose(0, 2, 1)
    mig = migration.T
    packed, zero = pack(h, ids, mig, tokens)
    received = exchange(packed)
    up_a = dequantize_up(up_values[0], up_scales[0] + zero[0, 0])
    down_a = dequantize_down(down_values[0], down_scales[0] + zero[0, 0])
    up_b = swapped(up_a)
    down_b = swapped(down_a)
    weights = mix_weights(h, ids, mig, gates)
    returned = exchange(expert(received, up_a, up_b, down_a, down_b))
    full, send = combine(h, weights, returned)
    return finish(h, full, swapped(send))


def solution(mesh):
    placed = (
        P(None, ("col", "row"), None),
        P(None, ("col", "row"), None),
        P(None, ("col", "row"), None),
        P(),
        P(("col", "row"), None, "pair"),
        P(("col", "row"), None, "pair"),
        P(("col", "row"), "pair", None),
        P(("col", "row"), "pair", None),
    )
    return jax.shard_map(
        per_device,
        mesh=mesh,
        in_specs=placed,
        out_specs=P(None, ("col", "row"), "pair"),
        check_vma=False,
    )
```

```python
import jax
import jax.numpy as jnp
from jax import lax
from jax.experimental import pallas as pl
from jax.experimental.pallas import tpu as pltpu
from jax.sharding import PartitionSpec as P

D = 2880
HALF = D // 2
HW2 = 768
E = 128
TOK = 64
TOP = 4
SUB = 8
LANES = 1152
THIRD = 384
WIDE = 1536
CHUNK = 384
BF = jnp.bfloat16
F32 = jnp.float32


def iota(shape, dim):
    return lax.broadcasted_iota(jnp.int32, shape, dim)


def one_hot(cond, dtype=BF):
    return jnp.where(cond, 1.0, 0.0).astype(dtype)


def dot(a, b, ca=1, cb=0):
    return lax.dot_general(a, b, (((ca,), (cb,)), ((), ())), preferred_element_type=F32)


def wanted(p, b, i):
    q = jnp.where(p < 6, p, 3 * (p - 6) + i)
    return jnp.where(b == (q & 1) + jnp.where(p < 6, 0, 2), (q >> 1) + 1, -1).astype(F32)


def placement(h, mig):
    named_from = one_hot(mig[0:1, :] == iota((E, mig.shape[1]), 0))
    named_to = one_hot(mig[1:2, :] == iota((E, mig.shape[1]), 0))
    moved = dot(named_from, named_to, 1, 1)
    named = dot(jnp.ones((SUB, mig.shape[1]), BF), named_to, 1, 1)[0:1, :]
    eye = one_hot(iota((E, E), 0) == iota((E, E), 1), F32)
    hf = h.astype(F32)
    return (moved * hf + eye * (1.0 - hf * named)).astype(BF)


def owners(ids):
    owner = jnp.zeros((E, TOK), F32)
    for k in range(TOP):
        owner = owner + one_hot(ids[k : k + 1, :] == iota((E, TOK), 0), F32)
    return owner.astype(BF)


def slot_codes(place, ids):
    named = dot(place, owners(ids)).astype(BF)
    earlier = one_hot(iota((TOK, TOK), 0) < iota((TOK, TOK), 1))
    rank = dot(named, earlier)
    return (named.astype(F32) * (rank + 1.0)).astype(BF)


def third(ref, i):
    return ref.at[:, i * THIRD : (i + 1) * THIRD]


def pack_body(h_ref, ids_ref, mig_ref, tok_ref, out_ref, zero_ref, tok, tail, rows, ids, mig, sems):
    h = h_ref[0]
    small = [
        pltpu.make_async_copy(ids_ref.at[h], ids, sems.at[4]),
        pltpu.make_async_copy(mig_ref, mig, sems.at[5]),
    ]
    for copy in small:
        copy.start()
    load = pltpu.make_async_copy(tok_ref.at[h], tok, sems.at[3])
    load.start()
    zero_ref[...] = jnp.zeros(zero_ref.shape, BF)
    for copy in small:
        copy.wait()
    owner = owners(ids[...])
    column = iota((TOK, 4 * TOK), 1) & (TOK - 1)
    token = iota((TOK, 4 * TOK), 0)
    codes = dot(owner, one_hot(token == column)) * (dot(owner, one_hot(token < column)) + 1.0)
    spread = one_hot((iota((E * SUB, E), 0) >> 3) == iota((E * SUB, E), 1))
    spread = dot(spread, placement(h, mig[...])).astype(BF)
    codes = dot(spread, codes.astype(BF)).reshape(E, SUB, 4 * TOK)
    p = iota((SUB, 4 * TOK), 0)
    b = iota((SUB, 4 * TOK), 1) >> 6
    load.wait()
    left = D - WIDE - LANES
    tail[:, 0:left] = tok[:, WIDE + LANES : D]
    tail[:, left:THIRD] = jnp.zeros((TOK, THIRD - left), BF)
    stores = []
    for i in range(3):
        select = one_hot(codes == wanted(p, b, i)[None]).reshape(E * SUB, 4 * TOK)
        source = jnp.concatenate(
            [
                tok[:, i * THIRD : (i + 1) * THIRD],
                tok[:, WIDE + i * THIRD : WIDE + (i + 1) * THIRD],
                tok[:, LANES:WIDE],
                tail[...],
            ],
            axis=0,
        )
        rows[:, i * THIRD : (i + 1) * THIRD] = dot(select, source).astype(BF)
        stores.append(pltpu.make_async_copy(third(rows, i), third(out_ref, i), sems.at[i]))
        stores[i].start()
    for store in stores:
        store.wait()


VMEM = pl.BlockSpec(memory_space=pltpu.VMEM)
SMEM = pl.BlockSpec(memory_space=pltpu.SMEM)
HBM = pl.BlockSpec(memory_space=pltpu.HBM)


def pack(h, ids, mig, tokens):
    return pl.pallas_call(
        pack_body,
        in_specs=[SMEM, HBM, HBM, HBM],
        out_specs=[HBM, VMEM],
        scratch_shapes=[
            pltpu.VMEM((TOK, D), BF),
            pltpu.VMEM((TOK, THIRD), BF),
            pltpu.VMEM((E * SUB, LANES), BF),
            pltpu.VMEM((TOP, TOK), jnp.int32),
            pltpu.VMEM(mig.shape, jnp.int32),
            pltpu.SemaphoreType.DMA((6,)),
        ],
        out_shape=[
            pltpu.HBM((E * SUB, LANES), BF),
            jax.ShapeDtypeStruct((16, 128), BF),
        ],
        name="pack",
        compiler_params=pltpu.CompilerParams(vmem_limit_bytes=24 << 20),
    )(h, in_hbm(ids), in_hbm(mig), in_hbm(tokens))


def mix_body(h_ref, ids_ref, mig_ref, gates_ref, out_ref):
    ids = ids_ref[h_ref[0]]
    gates = gates_ref[h_ref[0]]
    place = placement(h_ref[0], mig_ref[...])
    codes = slot_codes(place, ids)
    gate = jnp.zeros((E, TOK), F32)
    for k in range(TOP):
        gate = gate + jnp.where(ids[k : k + 1, :] == iota((E, TOK), 0), gates[k : k + 1, :], 0.0)
    repeat = one_hot((iota((4 * TOK, TOK), 0) & (TOK - 1)) == iota((4 * TOK, TOK), 1))
    spread = one_hot((iota((E, E * SUB), 1) >> 3) == iota((E, E * SUB), 0))

    def widened(x):
        return dot(dot(repeat, x, 1, 1).astype(BF), spread)

    codes = widened(codes)
    gate = widened(dot(place, gate.astype(BF)).astype(BF))
    p = iota((4 * TOK, E * SUB), 1) & (SUB - 1)
    b = iota((4 * TOK, E * SUB), 0) >> 6
    for i in range(3):
        part = jnp.where(codes == wanted(p, b, i), gate, 0.0).astype(BF)
        if i == 0:
            out_ref[3] = part[0 : 2 * TOK]
        out_ref[i] = part[2 * TOK : 4 * TOK]


def mix_weights(h, ids, mig, gates):
    return pl.pallas_call(
        mix_body,
        in_specs=[SMEM, VMEM, VMEM, VMEM],
        out_specs=VMEM,
        out_shape=jax.ShapeDtypeStruct((4, 2 * TOK, E * SUB), BF),
        name="mix_weights",
        compiler_params=pltpu.CompilerParams(vmem_limit_bytes=24 << 20),
    )(h, ids, mig, gates)


def pieces():
    for q in range(6):
        j, g = q // 2, q % 2
        for part in range(WIDE // 128):
            if part < 9:
                yield j, g * WIDE + part * 128, part, q
            else:
                yield j, g * WIDE + part * 128, 3 * (q % 3) + part - 9, 6 + q // 3


def expert_body(
    in_ref, up_a_hbm, up_b_hbm, down_a_hbm, down_b_hbm, out_hbm,
    wide, rows, hidden, out_ref, up_a, up_b, down_a, down_b, up_sems, down_sems, out_sems,
):
    ups, downs, stores = [], [], []
    for n, (src, dst) in enumerate(((up_a_hbm, up_a), (up_b_hbm, up_b))):
        for c in range(HW2 // CHUNK):
            cut = (slice(None), pl.ds(c * CHUNK, CHUNK))
            ups.append(pltpu.make_async_copy(src.at[cut], dst.at[cut], up_sems.at[len(ups)]))
    for n, (src, dst) in enumerate(((down_a_hbm, down_a), (down_b_hbm, down_b))):
        downs.append(pltpu.make_async_copy(src, dst, down_sems.at[n]))
    for load in ups + downs:
        load.start()
    for part in range(LANES // 128):
        wide[part] = in_ref[:, part * 128 : (part + 1) * 128].astype(F32)
    for j, lane, part, p in pieces():
        rows[j * E : (j + 1) * E, lane : lane + 128] = wide[part, pl.ds(p, E, stride=SUB), :].astype(BF)
    for n, up_ref in enumerate((up_a, up_b)):
        for c in range(HW2 // CHUNK):
            ups[n * (HW2 // CHUNK) + c].wait()
            pre = dot(rows[:, 0:D], up_ref[:, c * CHUNK : (c + 1) * CHUNK])
            act = pre * (0.5 + 0.5 * jnp.tanh(0.851 * pre))
            hidden[:, n * HW2 + c * CHUNK : n * HW2 + (c + 1) * CHUNK] = act.astype(BF)

    for load in downs:
        load.wait()

    def down(n0, n1):
        return dot(hidden[:, 0:HW2], down_a[n0:n1, :], 1, 1) + dot(hidden[:, HW2 : 2 * HW2], down_b[n0:n1, :], 1, 1)

    def put(y, g, i0, i1):
        for j in range(3):
            for part in range(3 * i0, 3 * i1):
                lane = (part - 3 * i0) * 128
                wide[part, pl.ds(2 * j + g, E, stride=SUB), :] = y[j * E : (j + 1) * E, lane : lane + 128]

    def send(i):
        for part in range(3 * i, 3 * i + 3):
            out_ref[:, part * 128 : (part + 1) * 128] = wide[part].astype(BF)
        stores.append(pltpu.make_async_copy(third(out_ref, i), third(out_hbm, i), out_sems.at[i]))
        stores[-1].start()

    for g in range(2):
        y = down(g * HALF + 2 * THIRD, (g + 1) * HALF)
        put(y, g, 2, 3)
        for j in range(3):
            q = 2 * j + g
            mine = y[j * E : (j + 1) * E, THIRD:]
            to = pl.ds(6 + q // 3, E, stride=SUB)
            wide[3 * (q % 3), to, :] = mine[:, 0:128]
            wide[3 * (q % 3) + 1, to, :] = mine[:, 128:256]
            last = jnp.concatenate([mine[:, 256:288], jnp.zeros((E, 96), F32)], axis=1)
            wide[3 * (q % 3) + 2, to, :] = last
    send(2)
    for g in range(2):
        put(down(g * HALF, g * HALF + 2 * THIRD), g, 0, 2)
    send(0)
    send(1)
    for store in stores:
        store.wait()


def in_hbm(x):
    return pltpu.with_memory_space_constraint(x, pltpu.HBM)


def on_chip(x):
    return pltpu.with_memory_space_constraint(x, pltpu.VMEM)


def expert(received, up_a, up_b, down_a, down_b):
    return pl.pallas_call(
        expert_body,
        in_specs=[VMEM, HBM, HBM, HBM, HBM],
        out_specs=HBM,
        scratch_shapes=[
            pltpu.VMEM((LANES // 128, E * SUB, 128), F32),
            pltpu.VMEM((3 * E, 2 * WIDE), BF),
            pltpu.VMEM((3 * E, 2 * HW2), BF),
            pltpu.VMEM((E * SUB, LANES), BF),
        ]
        + [pltpu.VMEM((D, HW2), BF)] * 4
        + [pltpu.SemaphoreType.DMA((2 * HW2 // CHUNK,)), pltpu.SemaphoreType.DMA((2,)), pltpu.SemaphoreType.DMA((3,))],
        out_shape=pltpu.HBM((E * SUB, LANES), BF),
        name="expert",
        compiler_params=pltpu.CompilerParams(vmem_limit_bytes=44 << 20),
    )(on_chip(received), *[in_hbm(x) for x in (up_a, up_b, down_a, down_b)])


def combine_body(h_ref, weights_ref, in_ref, full_ref, send_ref):
    h = h_ref[0]
    mains, tail = [], 0.0
    for i in range(3):
        pair = jnp.concatenate([weights_ref[3], weights_ref[i]], axis=0)
        out = dot(pair, in_ref[:, i * THIRD : (i + 1) * THIRD])
        mains.append(out[0 : 2 * TOK])
        tail = tail + out[2 * TOK : 4 * TOK]
    for g in range(2):
        own = slice(g * TOK, (g + 1) * TOK)

        def put(ref, own=own):
            for i in range(3):
                ref[:, i * THIRD : (i + 1) * THIRD] = mains[i][own].astype(BF)
            ref[:, LANES:HALF] = tail[own, 0 : HALF - LANES].astype(BF)

        @pl.when(h == g)
        def _():
            put(full_ref.at[g])

        @pl.when(h != g)
        def _():
            put(send_ref)


def combine(h, weights, returned):
    return pl.pallas_call(
        combine_body,
        in_specs=[SMEM, VMEM, VMEM],
        out_specs=[VMEM, VMEM],
        out_shape=[
            jax.ShapeDtypeStruct((2, TOK, HALF), BF),
            jax.ShapeDtypeStruct((TOK, HALF), BF),
        ],
        name="combine",
        compiler_params=pltpu.CompilerParams(vmem_limit_bytes=24 << 20),
    )(h, weights, on_chip(returned))


def finish_body(h_ref, full_ref, other_ref, out_ref, sem):
    copy = pltpu.make_async_copy(other_ref, out_ref.at[1 - h_ref[0]], sem)
    copy.start()
    copy.wait()


def finish(h, full, other):
    return pl.pallas_call(
        finish_body,
        in_specs=[SMEM, HBM, VMEM],
        out_specs=HBM,
        scratch_shapes=[pltpu.SemaphoreType.DMA(())],
        out_shape=jax.ShapeDtypeStruct(full.shape, BF),
        input_output_aliases={1: 0},
        name="finish",
    )(h, full, on_chip(other))


def exchange(x):
    blocks = x.reshape(E, SUB, LANES)
    return lax.all_to_all(blocks, ("col", "row"), 0, 0, tiled=True).reshape(E * SUB, LANES)


def swapped(x):
    return lax.ppermute(x, "pair", [(0, 1), (1, 0)])


def dequantize_up(values, scales):
    shaped = values.reshape(D // 32, 32, HW2).astype(F32) * scales.astype(F32)[:, None, :]
    return shaped.astype(BF).reshape(D, HW2)


def dequantize_down(values, scales):
    group = (iota((HW2 // 32, HW2), 1) // 32 == iota((HW2 // 32, HW2), 0)).astype(BF)
    spread = jnp.einsum("bn,bk->nk", scales, group, preferred_element_type=F32)
    return (values.T.astype(F32) * spread).astype(BF)


def per_device(
    tokens, expert_ids, gate_weights, migration, up_values, up_scales, down_values, down_scales
):
    own = lax.axis_index("pair")
    h = own.astype(jnp.int32).reshape(1)
    ids = expert_ids.transpose(0, 2, 1)
    gates = gate_weights.transpose(0, 2, 1)
    mig = migration.T
    packed, zero = pack(h, ids, mig, tokens)
    received = exchange(packed)
    up_a = dequantize_up(up_values[0], up_scales[0] + zero[0, 0])
    down_a = dequantize_down(down_values[0], down_scales[0] + zero[0, 0])
    up_b = swapped(up_a)
    down_b = swapped(down_a)
    weights = mix_weights(h, ids, mig, gates)
    returned = exchange(expert(received, up_a, up_b, down_a, down_b))
    full, send = combine(h, weights, returned)
    return finish(h, full, swapped(send))


def solution(mesh):
    placed = (
        P(None, ("col", "row"), None),
        P(None, ("col", "row"), None),
        P(None, ("col", "row"), None),
        P(),
        P(("col", "row"), None, "pair"),
        P(("col", "row"), None, "pair"),
        P(("col", "row"), "pair", None),
        P(("col", "row"), "pair", None),
    )
    return jax.shard_map(
        per_device,
        mesh=mesh,
        in_specs=placed,
        out_specs=P(None, ("col", "row"), "pair"),
        check_vma=False,
    )
```

```python
import jax
import jax.numpy as jnp
from jax import lax
from jax.experimental import pallas as pl
from jax.experimental.pallas import tpu as pltpu
from jax.sharding import PartitionSpec as P


D = 2880
HALF = D // 2
HW2 = 768
E = 128
TOK = 64
TOP = 4
SUB = 8
LANES = 1152
THIRD = 384
MAIN = 2176
GROUPS = 640
CHUNK = 384
BF = jnp.bfloat16
F32 = jnp.float32


def iota(shape, dim):
    return lax.broadcasted_iota(jnp.int32, shape, dim)


def one_hot(cond, dtype=BF):
    return jnp.where(cond, 1.0, 0.0).astype(dtype)


def dot(a, b, ca=1, cb=0):
    return lax.dot_general(a, b, (((ca,), (cb,)), ((), ())), preferred_element_type=F32)


def wanted(p, b, i):
    q = jnp.where(p < 6, p, 3 * (p - 6) + i)
    return jnp.where(b == (q & 1) + jnp.where(p < 6, 0, 2), (q >> 1) + 1, -1).astype(F32)


def placement(h, mig):
    named_from = one_hot(mig[0:1, :] == iota((E, mig.shape[1]), 0))
    named_to = one_hot(mig[1:2, :] == iota((E, mig.shape[1]), 0))
    moved = dot(named_from, named_to, 1, 1)
    named = dot(jnp.ones((SUB, mig.shape[1]), BF), named_to, 1, 1)[0:1, :]
    eye = one_hot(iota((E, E), 0) == iota((E, E), 1), F32)
    hf = h.astype(F32)
    return (moved * hf + eye * (1.0 - hf * named)).astype(BF)


def owners(ids):
    owner = jnp.zeros((E, TOK), F32)
    for k in range(TOP):
        owner = owner + one_hot(ids[k : k + 1, :] == iota((E, TOK), 0), F32)
    return owner.astype(BF)


def slot_codes(place, ids):
    named = dot(place, owners(ids)).astype(BF)
    earlier = one_hot(iota((TOK, TOK), 0) < iota((TOK, TOK), 1))
    rank = dot(named, earlier)
    return (named.astype(F32) * (rank + 1.0)).astype(BF)


def third(ref, i):
    return ref.at[:, i * THIRD : (i + 1) * THIRD]


def pack_body(h_ref, ids_ref, mig_ref, tok_ref, out_ref, zero_ref, tok, source, rows, ids, mig, sems):
    h = h_ref[0]
    small = [
        pltpu.make_async_copy(ids_ref.at[h], ids, sems.at[4]),
        pltpu.make_async_copy(mig_ref, mig, sems.at[5]),
    ]
    for copy in small:
        copy.start()
    load = pltpu.make_async_copy(tok_ref.at[h], tok, sems.at[3])
    load.start()
    zero_ref[...] = jnp.zeros(zero_ref.shape, BF)
    source[TOK:, :] = jnp.zeros((3 * TOK, MAIN), BF)
    for copy in small:
        copy.wait()
    owner = owners(ids[...])
    column = iota((TOK, 4 * TOK), 1) & (TOK - 1)
    token = iota((TOK, 4 * TOK), 0)
    codes = dot(owner, one_hot(token == column)) * (dot(owner, one_hot(token < column)) + 1.0)
    spread = one_hot((iota((E * 4, E), 0) >> 2) == iota((E * 4, E), 1))
    spread = dot(spread, placement(h, mig[...])).astype(BF)
    codes = dot(spread, codes.astype(BF)).reshape(E // 2, SUB, 4 * TOK)
    q = iota((SUB, 4 * TOK), 0) & 3
    b = iota((SUB, 4 * TOK), 1) >> 6
    want = jnp.where(q < 3, jnp.where(b == 0, q + 1, -1), jnp.where(b > 0, b, -1)).astype(F32)
    select = one_hot(codes == want[None]).reshape(E * 4, 4 * TOK)
    load.wait()
    source[0:TOK, :] = tok[:, 0:MAIN]
    piece = tok[:, MAIN + GROUPS : D]
    for j in range(3):
        mine = slice((j + 1) * TOK, (j + 2) * TOK)
        source[mine, j * GROUPS : (j + 1) * GROUPS] = tok[:, MAIN : MAIN + GROUPS]
    source[TOK : 2 * TOK, 3 * GROUPS : 3 * GROUPS + 64] = piece
    shifted = jnp.concatenate([jnp.zeros((TOK, 64), F32), piece.astype(F32)], axis=1)
    source[2 * TOK : 3 * TOK, 3 * GROUPS : 3 * GROUPS + 128] = shifted.astype(BF)
    source[3 * TOK : 4 * TOK, 3 * GROUPS + 128 : 3 * GROUPS + 192] = piece
    stores = []
    for n, (c0, c1) in enumerate(((0, 768), (768, 1536), (1536, MAIN))):
        part = dot(select, source[:, c0:c1]).astype(BF)
        rows[:, :, c0:c1] = part.reshape(E, 4, c1 - c0)
        cut = (slice(None), slice(None), pl.ds(c0, c1 - c0))
        stores.append(pltpu.make_async_copy(rows.at[cut], out_ref.at[cut], sems.at[n]))
        stores[n].start()
    for store in stores:
        store.wait()


VMEM = pl.BlockSpec(memory_space=pltpu.VMEM)
SMEM = pl.BlockSpec(memory_space=pltpu.SMEM)
HBM = pl.BlockSpec(memory_space=pltpu.HBM)


def pack(h, ids, mig, tokens):
    return pl.pallas_call(
        pack_body,
        in_specs=[SMEM, HBM, HBM, HBM],
        out_specs=[HBM, VMEM],
        scratch_shapes=[
            pltpu.VMEM((TOK, D), BF),
            pltpu.VMEM((4 * TOK, MAIN), BF),
            pltpu.VMEM((E, 4, MAIN), BF),
            pltpu.VMEM((TOP, TOK), jnp.int32),
            pltpu.VMEM(mig.shape, jnp.int32),
            pltpu.SemaphoreType.DMA((6,)),
        ],
        out_shape=[
            pltpu.HBM((E, 4, MAIN), BF),
            jax.ShapeDtypeStruct((16, 128), BF),
        ],
        name="pack",
        compiler_params=pltpu.CompilerParams(vmem_limit_bytes=24 << 20),
    )(h, in_hbm(ids), in_hbm(mig), in_hbm(tokens))


def mix_body(h_ref, ids_ref, mig_ref, gates_ref, out_ref):
    ids = ids_ref[h_ref[0]]
    gates = gates_ref[h_ref[0]]
    place = placement(h_ref[0], mig_ref[...])
    codes = slot_codes(place, ids)
    gate = jnp.zeros((E, TOK), F32)
    for k in range(TOP):
        gate = gate + jnp.where(ids[k : k + 1, :] == iota((E, TOK), 0), gates[k : k + 1, :], 0.0)
    repeat = one_hot((iota((4 * TOK, TOK), 0) & (TOK - 1)) == iota((4 * TOK, TOK), 1))
    spread = one_hot((iota((E, E * SUB), 1) >> 3) == iota((E, E * SUB), 0))

    def widened(x):
        return dot(dot(repeat, x, 1, 1).astype(BF), spread)

    codes = widened(codes)
    gate = widened(dot(place, gate.astype(BF)).astype(BF))
    p = iota((4 * TOK, E * SUB), 1) & (SUB - 1)
    b = iota((4 * TOK, E * SUB), 0) >> 6
    for i in range(3):
        part = jnp.where(codes == wanted(p, b, i), gate, 0.0).astype(BF)
        if i == 0:
            out_ref[3] = part[0 : 2 * TOK]
        out_ref[i] = part[2 * TOK : 4 * TOK]


def mix_weights(h, ids, mig, gates):
    return pl.pallas_call(
        mix_body,
        in_specs=[SMEM, VMEM, VMEM, VMEM],
        out_specs=VMEM,
        out_shape=jax.ShapeDtypeStruct((4, 2 * TOK, E * SUB), BF),
        name="mix_weights",
        compiler_params=pltpu.CompilerParams(vmem_limit_bytes=24 << 20),
    )(h, ids, mig, gates)


def expert_body(
    in_ref, up_a_hbm, up_b_hbm, down_a_hbm, down_b_hbm, out_hbm,
    wide, wide_in, rows, hidden, out_ref, up_a, up_b, down_a, down_b, up_sems, down_sems, out_sems,
):
    ups, downs, stores = [], [], []
    for src, dst in ((up_a_hbm, up_a), (up_b_hbm, up_b)):
        for c in range(HW2 // CHUNK):
            cut = (slice(None), pl.ds(c * CHUNK, CHUNK))
            ups.append(pltpu.make_async_copy(src.at[cut], dst.at[cut], up_sems.at[len(ups)]))
    for n, (src, dst) in enumerate(((down_a_hbm, down_a), (down_b_hbm, down_b))):
        downs.append(pltpu.make_async_copy(src, dst, down_sems.at[n]))
    for load in ups + downs:
        load.start()
    for part in range(MAIN // 128):
        lanes = in_ref[:, :, part * 128 : (part + 1) * 128].astype(F32)
        wide_in[part] = lanes.reshape(4 * E, 128)
    last = MAIN // 128 - 2
    halves = ((last, 0), (last, 64), (last + 1, 0))
    for j in range(3):
        mine = slice(j * E, (j + 1) * E)
        for part in range(MAIN // 128):
            rows[mine, part * 128 : (part + 1) * 128] = wide_in[part, pl.ds(j, E, stride=4), :].astype(BF)
        for part in range(GROUPS // 128):
            lane = MAIN + part * 128
            found = wide_in[j * (GROUPS // 128) + part, pl.ds(3, E, stride=4), :]
            rows[mine, lane : lane + 128] = found.astype(BF)
        part, lane = halves[j]
        rows[mine, MAIN + GROUPS : D] = wide_in[part, pl.ds(3, E, stride=4), :][:, lane : lane + 64].astype(BF)
    for n, up_ref in enumerate((up_a, up_b)):
        for c in range(HW2 // CHUNK):
            ups[n * (HW2 // CHUNK) + c].wait()
            pre = dot(rows[:, 0:D], up_ref[:, c * CHUNK : (c + 1) * CHUNK])
            act = pre * (0.5 + 0.5 * jnp.tanh(0.851 * pre))
            hidden[:, n * HW2 + c * CHUNK : n * HW2 + (c + 1) * CHUNK] = act.astype(BF)

    for load in downs:
        load.wait()

    def down(n0, n1):
        return dot(hidden[:, 0:HW2], down_a[n0:n1, :], 1, 1) + dot(hidden[:, HW2 : 2 * HW2], down_b[n0:n1, :], 1, 1)

    def put(y, g, i0, i1):
        for j in range(3):
            for part in range(3 * i0, 3 * i1):
                lane = (part - 3 * i0) * 128
                wide[part, pl.ds(2 * j + g, E, stride=SUB), :] = y[j * E : (j + 1) * E, lane : lane + 128]

    def send(i):
        for part in range(3 * i, 3 * i + 3):
            out_ref[:, part * 128 : (part + 1) * 128] = wide[part].astype(BF)
        stores.append(pltpu.make_async_copy(third(out_ref, i), third(out_hbm, i), out_sems.at[i]))
        stores[-1].start()

    for g in range(2):
        y = down(g * HALF + 2 * THIRD, (g + 1) * HALF)
        put(y, g, 2, 3)
        for j in range(3):
            q = 2 * j + g
            mine = y[j * E : (j + 1) * E, THIRD:]
            to = pl.ds(6 + q // 3, E, stride=SUB)
            wide[3 * (q % 3), to, :] = mine[:, 0:128]
            wide[3 * (q % 3) + 1, to, :] = mine[:, 128:256]
            last = jnp.concatenate([mine[:, 256:288], jnp.zeros((E, 96), F32)], axis=1)
            wide[3 * (q % 3) + 2, to, :] = last
    send(2)
    for g in range(2):
        put(down(g * HALF, g * HALF + 2 * THIRD), g, 0, 2)
    send(0)
    send(1)
    for store in stores:
        store.wait()


def in_hbm(x):
    return pltpu.with_memory_space_constraint(x, pltpu.HBM)


def on_chip(x):
    return pltpu.with_memory_space_constraint(x, pltpu.VMEM)


def expert(received, up_a, up_b, down_a, down_b):
    return pl.pallas_call(
        expert_body,
        in_specs=[VMEM, HBM, HBM, HBM, HBM],
        out_specs=HBM,
        scratch_shapes=[
            pltpu.VMEM((LANES // 128, E * SUB, 128), F32),
            pltpu.VMEM((MAIN // 128, 4 * E, 128), F32),
            pltpu.VMEM((3 * E, D), BF),
            pltpu.VMEM((3 * E, 2 * HW2), BF),
            pltpu.VMEM((E * SUB, LANES), BF),
        ]
        + [pltpu.VMEM((D, HW2), BF)] * 4
        + [pltpu.SemaphoreType.DMA((2 * HW2 // CHUNK,)), pltpu.SemaphoreType.DMA((2,)), pltpu.SemaphoreType.DMA((3,))],
        out_shape=pltpu.HBM((E * SUB, LANES), BF),
        name="expert",
        compiler_params=pltpu.CompilerParams(vmem_limit_bytes=44 << 20),
    )(on_chip(received), *[in_hbm(x) for x in (up_a, up_b, down_a, down_b)])


def combine_body(h_ref, weights_ref, in_ref, full_ref, send_ref):
    h = h_ref[0]
    mains, tail = [], 0.0
    for i in range(3):
        pair = jnp.concatenate([weights_ref[3], weights_ref[i]], axis=0)
        out = dot(pair, in_ref[:, i * THIRD : (i + 1) * THIRD])
        mains.append(out[0 : 2 * TOK])
        tail = tail + out[2 * TOK : 4 * TOK]
    for g in range(2):
        own = slice(g * TOK, (g + 1) * TOK)

        def put(ref, own=own):
            for i in range(3):
                ref[:, i * THIRD : (i + 1) * THIRD] = mains[i][own].astype(BF)
            ref[:, LANES:HALF] = tail[own, 0 : HALF - LANES].astype(BF)

        @pl.when(h == g)
        def _():
            put(full_ref.at[g])

        @pl.when(h != g)
        def _():
            put(send_ref)


def combine(h, weights, returned):
    return pl.pallas_call(
        combine_body,
        in_specs=[SMEM, VMEM, VMEM],
        out_specs=[VMEM, VMEM],
        out_shape=[
            jax.ShapeDtypeStruct((2, TOK, HALF), BF),
            jax.ShapeDtypeStruct((TOK, HALF), BF),
        ],
        name="combine",
        compiler_params=pltpu.CompilerParams(vmem_limit_bytes=24 << 20),
    )(h, weights, on_chip(returned))


def finish_body(h_ref, full_ref, other_ref, out_ref, sem):
    copy = pltpu.make_async_copy(other_ref, out_ref.at[1 - h_ref[0]], sem)
    copy.start()
    copy.wait()


def finish(h, full, other):
    return pl.pallas_call(
        finish_body,
        in_specs=[SMEM, HBM, VMEM],
        out_specs=HBM,
        scratch_shapes=[pltpu.SemaphoreType.DMA(())],
        out_shape=jax.ShapeDtypeStruct(full.shape, BF),
        input_output_aliases={1: 0},
        name="finish",
    )(h, full, on_chip(other))


def exchange(blocks):
    return lax.all_to_all(blocks, ("col", "row"), 0, 0, tiled=True)


def swapped(x):
    return lax.ppermute(x, "pair", [(0, 1), (1, 0)])


def dequantize_up(values, scales):
    shaped = values.reshape(D // 32, 32, HW2).astype(F32) * scales.astype(F32)[:, None, :]
    return shaped.astype(BF).reshape(D, HW2)


def dequantize_down(values, scales):
    group = (iota((HW2 // 32, HW2), 1) // 32 == iota((HW2 // 32, HW2), 0)).astype(BF)
    spread = jnp.einsum("bn,bk->nk", scales, group, preferred_element_type=F32)
    return (values.T.astype(F32) * spread).astype(BF)


def per_device(
    tokens, expert_ids, gate_weights, migration, up_values, up_scales, down_values, down_scales
):
    own = lax.axis_index("pair")
    h = own.astype(jnp.int32).reshape(1)
    ids = expert_ids.transpose(0, 2, 1)
    gates = gate_weights.transpose(0, 2, 1)
    mig = migration.T
    packed, zero = pack(h, ids, mig, tokens)
    received = exchange(packed)
    up_a = dequantize_up(up_values[0], up_scales[0] + zero[0, 0])
    down_a = dequantize_down(down_values[0], down_scales[0] + zero[0, 0])
    up_b = swapped(up_a)
    down_b = swapped(down_a)
    weights = mix_weights(h, ids, mig, gates)
    results = expert(received, up_a, up_b, down_a, down_b).reshape(E, SUB, LANES)
    returned = exchange(results).reshape(E * SUB, LANES)
    full, send = combine(h, weights, returned)
    return finish(h, full, swapped(send))


def solution(mesh):
    placed = (
        P(None, ("col", "row"), None),
        P(None, ("col", "row"), None),
        P(None, ("col", "row"), None),
        P(),
        P(("col", "row"), None, "pair"),
        P(("col", "row"), None, "pair"),
        P(("col", "row"), "pair", None),
        P(("col", "row"), "pair", None),
    )
    return jax.shard_map(
        per_device,
        mesh=mesh,
        in_specs=placed,
        out_specs=P(None, ("col", "row"), "pair"),
        check_vma=False,
    )
```
